32 devices in a mesh: island: 2 (over core), dp: 4 (over z), tensor: 4 (over y, x).
Axes of the slice: x: 2, y: 2, z: 4, core: 2. Of those that a mesh axis runs over, the one named last changes fastest.
Arguments:
- pseudo_grad: float32 [2, 48, 256, 5120], P('island', None, 'dp', 'tensor'), may hold values from -1000 to 1000, as said below
- block_owner: int32 [48], replicated, may hold values from 0 to 7, as said below
Outputs:
- update: bfloat16 [8, 12, 256, 5120], P(('island', 'dp'), None, None, 'tensor')
The draws below stay inside these ranges and needn't reach their ends.
Inputs may be any that keep to these rules, and one draw needn't show every extreme that they name: `pseudo_grad`: float pseudo-gradients; entries lie within the range. `block_owner`: every owner holds at most 12 blocks and at least one; some owner holds exactly 12.
All inputs are finite; a program needn't handle non-finite values.
Results may differ from the reference program's by a relative error of at most 0.001.
Values sent between devices are 32-bit elements; how exact they have to be, the bound alone decides.
A program may use at most 128 MiB of HBM per device.

```python
import math
import jax
import jax.numpy as jnp
from jax import lax

D = 5120
HB = 256
ISLANDS = 2
OWNERS = 8
BLOCKS = 48
SLOTS = 12


def draw_pseudo_grad(key, part):
    shape = (ISLANDS, BLOCKS, HB, D)
    keys = jax.random.split(jax.random.fold_in(key, 11), 3)
    trend = jnp.exp(math.log(3.0) * jnp.arange(D, dtype=jnp.float32) / (D - 1))
    col_scale = jnp.exp(jax.random.uniform(keys[1], (1, 1, 1, D), jnp.float32, 0.0, math.log(10.0 / 3.0))) * trend
    row_scale = jnp.exp(jax.random.uniform(keys[0], (1, BLOCKS, HB, 1), jnp.float32, 0.0, math.log(10.0)))
    base = jax.random.truncated_normal(keys[2], -4.0, 4.0, shape, jnp.float32)
    return (base * row_scale * col_scale).astype(jnp.float32)


def draw_block_owner(key, part):
    keys = jax.random.split(jax.random.fold_in(key, 23), 2)
    average = BLOCKS // OWNERS
    quarter = OWNERS // 4
    ranking = jnp.arange(OWNERS, dtype=jnp.int32)
    sorted_counts = jnp.where(ranking < quarter, 2 * average, jnp.where(ranking < 2 * quarter, average, average // 2))
    shuffle = jax.random.permutation(keys[0], OWNERS)
    counts = sorted_counts[shuffle]
    owner_list = jnp.repeat(ranking, counts, total_repeat_length=BLOCKS)
    reorder = jax.random.permutation(keys[1], BLOCKS)
    return owner_list[reorder].astype(jnp.int32)


def setup_inputs(seed: int = 0) -> dict:
    key_list = jax.random.split(jax.random.key(seed), 3)
    return {
        "pseudo_grad": draw_pseudo_grad(jax.random.fold_in(key_list[2], 71), 0),
        "block_owner": draw_block_owner(jax.random.fold_in(key_list[2], 71), 0),
    }


COEF_A = 3.4445
COEF_B = -4.775
COEF_C = 2.0315
EPSILON = 1e-07

def slot_table(block_owner, owner_count, slot_count):
    blocks = block_owner.shape[0]
    positions = jnp.arange(blocks, dtype=jnp.int32)
    one_hot = (block_owner[:, None] == jnp.arange(owner_count, dtype=jnp.int32)[None, :]).astype(jnp.float32)
    earlier = (positions[None, :] < positions[:, None]).astype(jnp.float32)
    counts_before = jnp.dot(earlier, one_hot, precision=lax.Precision.HIGHEST)
    slot = lax.optimization_barrier(jnp.sum(counts_before * one_hot, axis=1)).astype(jnp.int32)
    slot_key = block_owner * slot_count + slot
    entries = jnp.arange(owner_count * slot_count, dtype=jnp.int32)
    matches = slot_key[None, :] == entries[:, None]
    slot_index = lax.optimization_barrier(jnp.sum(jnp.where(matches, positions[None, :], 0), axis=1)).astype(jnp.int32)
    slot_valid = jnp.any(matches, axis=1)
    return (slot_index, slot_valid)

def newton(block):
    norm_value = jnp.sqrt(jnp.sum(block * block))
    iterate = block / (norm_value + EPSILON)
    for sweep in range(2):
        gram_mat = jnp.dot(iterate, iterate.T, precision=lax.Precision.HIGHEST)
        poly_mat = COEF_B * gram_mat + COEF_C * jnp.dot(gram_mat, gram_mat, precision=lax.Precision.HIGHEST)
        iterate = COEF_A * iterate + jnp.dot(poly_mat, iterate, precision=lax.Precision.HIGHEST)
    return (math.sqrt(D) * iterate).astype(jnp.bfloat16)

def reference(pseudo_grad, block_owner):

    def one_block(block_id):
        total = lax.optimization_barrier(jnp.sum(pseudo_grad[:, block_id], axis=0))
        return newton(total)
    results = lax.map(one_block, jnp.arange(BLOCKS, dtype=jnp.int32))
    slot_index, slot_valid = slot_table(block_owner, OWNERS, SLOTS)
    placed = jnp.where(slot_valid[:, None, None], results[slot_index].astype(jnp.float32), 0.0)
    return placed.astype(jnp.bfloat16).reshape(OWNERS, SLOTS, HB, D)
```

```python
import functools
import math

import jax
import jax.numpy as jnp
from jax import lax
from jax.experimental import pallas as pl
from jax.experimental.pallas import tpu as pltpu
from jax.sharding import PartitionSpec as P

COEF_A = 3.4445
COEF_B = -4.775
COEF_C = 2.0315
EPSILON = 1e-07
PREC = lax.Precision.HIGH


def batch_dot(left, right):
    return jnp.einsum("khg,kgc->khc", left, right, precision=PREC)


def polynomial(gram_mat):
    return COEF_B * gram_mat + COEF_C * batch_dot(gram_mat, gram_mat)


def orthogonalize(blocks, width):
    partial_value = jnp.einsum("khc,kgc->khg", blocks, blocks, precision=PREC)
    gram_first = lax.psum(partial_value, "tensor")
    squares = jnp.trace(gram_first, axis1=1, axis2=2)
    inverse = 1.0 / (jnp.sqrt(squares) + EPSILON)
    gram_start = gram_first * (inverse * inverse)[:, None, None]
    poly_first = polynomial(gram_start)
    identity = jnp.eye(blocks.shape[1], dtype=jnp.float32)[None]
    first_factor = COEF_A * identity + poly_first
    gram_second = batch_dot(batch_dot(first_factor, gram_start), first_factor)
    second_factor = COEF_A * identity + polynomial(gram_second)
    factor = batch_dot(second_factor, first_factor) * inverse[:, None, None]
    final = batch_dot(factor, blocks)
    return (math.sqrt(width) * final).astype(jnp.bfloat16)[None]


def rank_before(key):
    positions = jnp.arange(key.shape[0], dtype=jnp.int32)
    same = (key[None, :] == key[:, None]) & (positions[None, :] < positions[:, None])
    return jnp.sum(same.astype(jnp.int32), axis=1)


def invert(target, count):
    positions = jnp.arange(target.shape[0], dtype=jnp.int32)
    matches = target[None, :] == jnp.arange(count, dtype=jnp.int32)[:, None]
    return jnp.sum(jnp.where(matches, positions[None, :], 0), axis=1), jnp.any(matches, axis=1)


def pack_kernel(group, index_ref, half_ref, *refs):
    out_ref = refs[-1]
    for g in range(group):
        out_ref[g] = refs[2 * g][0] + refs[2 * g + 1][0]


def pack(own_grad, other, index, island):
    count = index.shape[0]
    rows, half = other.shape[1], other.shape[2]
    group = max(g for g in range(1, 7) if count % g == 0)
    specs = []
    for g in range(group):
        specs.append(pl.BlockSpec((1, rows, half), lambda i, ix, h, g=g: (ix[i * group + g], 0, h[0])))
        specs.append(pl.BlockSpec((1, rows, half), lambda i, ix, h, g=g: (ix[i * group + g], 0, 0)))
    return pl.pallas_call(
        functools.partial(pack_kernel, group),
        grid_spec=pltpu.PrefetchScalarGridSpec(
            num_scalar_prefetch=2,
            grid=(count // group,),
            in_specs=specs,
            out_specs=pl.BlockSpec((group, rows, half), lambda i, ix, h: (i, 0, 0)),
        ),
        out_shape=jax.ShapeDtypeStruct((count, rows, half), jnp.float32),
        compiler_params=pltpu.CompilerParams(vmem_limit_bytes=48 * 2**20),
    )(index, island.reshape(1), *([own_grad, other] * group))


def transport_kernel(n, chunk, chunks, send_ref, a_ref, b_ref, stage, local_sem, send_sem, recv_sem, relay_send, relay_recv):
    me = lax.axis_index("dp")
    partner = 1 - lax.axis_index("island")
    barrier = pltpu.get_barrier_semaphore()
    for d in range(1, n):
        pl.semaphore_signal(barrier, inc=1, device_id={"dp": lax.rem(me + d, n)}, device_id_type=pl.DeviceIdType.MESH)
    pl.semaphore_signal(barrier, inc=1, device_id={"island": partner}, device_id_type=pl.DeviceIdType.MESH)
    pl.semaphore_wait(barrier, n)

    def remote(c, d):
        peer = lax.rem(me + d, n)
        span = pl.ds(c * chunk, chunk)
        return pltpu.make_async_remote_copy(
            src_ref=send_ref.at[peer, span],
            dst_ref=a_ref.at[span, me],
            send_sem=send_sem.at[c, d],
            recv_sem=recv_sem.at[c, d],
            device_id={"dp": peer},
            device_id_type=pl.DeviceIdType.MESH,
        )

    def relay(c):
        span = pl.ds(c * chunk, chunk)
        return pltpu.make_async_remote_copy(
            src_ref=a_ref.at[span],
            dst_ref=b_ref.at[span],
            send_sem=relay_send.at[c],
            recv_sem=relay_recv.at[c],
            device_id={"island": partner},
            device_id_type=pl.DeviceIdType.MESH,
        )

    def start(c, carry):
        for d in range(1, n):
            remote(c, d).start()
        return carry

    lax.fori_loop(0, chunks, start, 0)
    load = pltpu.make_async_copy(send_ref.at[me], stage, local_sem.at[0])
    load.start()
    load.wait()
    store = pltpu.make_async_copy(stage, a_ref.at[pl.ds(0, chunk * chunks), me], local_sem.at[1])
    store.start()
    store.wait()

    def arrive(c, carry):
        for d in range(1, n):
            remote(c, d).wait_recv()
        relay(c).start()
        return carry

    lax.fori_loop(0, chunks, arrive, 0)

    def finish(c, carry):
        for d in range(1, n):
            remote(c, d).wait_send()
        relay(c).wait()
        return carry

    lax.fori_loop(0, chunks, finish, 0)


def transport(send, most, chunk, collective_id):
    n, count, rows, half = send.shape
    chunks = count // chunk
    shape = jax.ShapeDtypeStruct((most, n, rows, half), jnp.float32)
    return pl.pallas_call(
        functools.partial(transport_kernel, n, chunk, chunks),
        out_shape=(shape, shape),
        in_specs=[pl.BlockSpec(memory_space=pl.ANY)],
        out_specs=(pl.BlockSpec(memory_space=pl.ANY), pl.BlockSpec(memory_space=pl.ANY)),
        scratch_shapes=[
            pltpu.VMEM((count, rows, half), jnp.float32),
            pltpu.SemaphoreType.DMA((2,)),
            pltpu.SemaphoreType.DMA((chunks, n)),
            pltpu.SemaphoreType.DMA((chunks, n)),
            pltpu.SemaphoreType.DMA((chunks,)),
            pltpu.SemaphoreType.DMA((chunks,)),
        ],
        compiler_params=pltpu.CompilerParams(collective_id=collective_id, has_side_effects=True),
    )(send)


def body(pseudo_grad, block_owner):
    own_grad = pseudo_grad[0]
    blocks, rows, columns = own_grad.shape
    half = columns // 2
    dp_count = lax.axis_size("dp")
    island_count = lax.axis_size("island")
    owner_count = island_count * dp_count
    slot_count = 2 * (blocks // owner_count)
    most = island_count * slot_count
    least = blocks // dp_count
    chunk = max(1, slot_count // 4)
    island = lax.axis_index("island")
    device_dp = lax.axis_index("dp")

    slot = rank_before(block_owner)
    chip = lax.rem(block_owner, dp_count)
    chip_slot = rank_before(chip)
    send_index, _ = invert(chip * most + chip_slot, dp_count * most)
    send_index = send_index.reshape(dp_count, most)
    needed = jnp.max(chip_slot) + 1
    own_index, own_valid = invert(block_owner * slot_count + slot, owner_count * slot_count)
    base = (island * dp_count + device_dp) * slot_count
    own_block = lax.dynamic_slice_in_dim(own_index, base, slot_count)
    own_valid = lax.dynamic_slice_in_dim(own_valid, base, slot_count)
    own_place = chip_slot[own_block]

    theirs = lax.dynamic_slice_in_dim(own_grad, (1 - island) * half, half, axis=2)
    other = lax.ppermute(theirs, "island", [(0, 1), (1, 0)])

    counts = [c for c in range(chunk, most + 1, chunk) if c >= least]

    def branch(count, number):
        def run(own_grad, other):
            packed = pack(own_grad, other, send_index[:, :count].reshape(-1), island)
            return transport(packed.reshape(dp_count, count, rows, half), most, chunk, number)
        return run

    choice = jnp.sum((needed > jnp.array(counts, dtype=jnp.int32)).astype(jnp.int32))
    mine, partner = lax.switch(choice, [branch(c, i) for i, c in enumerate(counts)], own_grad, other)
    mine = jnp.take(mine, own_place, axis=0).reshape(slot_count, dp_count * rows, half)
    partner = jnp.take(partner, own_place, axis=0).reshape(slot_count, dp_count * rows, half)
    first = island == 0
    picked = jnp.concatenate([jnp.where(first, mine, partner), jnp.where(first, partner, mine)], axis=2)
    picked = jnp.where(own_valid[:, None, None], picked, 0.0)
    return orthogonalize(picked, columns * lax.axis_size("tensor"))


def solution(mesh):
    in_specs = (P("island", None, "dp", "tensor"), P())
    out_specs = P(("island", "dp"), None, None, "tensor")
    return jax.shard_map(body, mesh=mesh, in_specs=in_specs, out_specs=out_specs, check_vma=False)
```

```python
import functools
import math

import jax
import jax.numpy as jnp
from jax import lax
from jax.experimental import pallas as pl
from jax.experimental.pallas import tpu as pltpu
from jax.sharding import PartitionSpec as P

COEF_A = 3.4445
COEF_B = -4.775
COEF_C = 2.0315
EPSILON = 1e-07


def rank_before(key):
    positions = jnp.arange(key.shape[0], dtype=jnp.int32)
    same = (key[None, :] == key[:, None]) & (positions[None, :] < positions[:, None])
    return jnp.sum(same.astype(jnp.int32), axis=1)


def invert(target, count):
    positions = jnp.arange(target.shape[0], dtype=jnp.int32)
    matches = target[None, :] == jnp.arange(count, dtype=jnp.int32)[:, None]
    return jnp.sum(jnp.where(matches, positions[None, :], 0), axis=1), jnp.any(matches, axis=1)


def pack_kernel(group, index_ref, half_ref, *refs):
    out_ref = refs[-1]
    for g in range(group):
        out_ref[g] = refs[2 * g][0] + refs[2 * g + 1][0]


def pack(own_grad, other, index, island):
    count = index.shape[0]
    rows, half = other.shape[1], other.shape[2]
    group = max(g for g in range(1, 7) if count % g == 0)
    specs = []
    for g in range(group):
        specs.append(pl.BlockSpec((1, rows, half), lambda i, ix, h, g=g: (ix[i * group + g], 0, h[0])))
        specs.append(pl.BlockSpec((1, rows, half), lambda i, ix, h, g=g: (ix[i * group + g], 0, 0)))
    return pl.pallas_call(
        functools.partial(pack_kernel, group),
        grid_spec=pltpu.PrefetchScalarGridSpec(
            num_scalar_prefetch=2,
            grid=(count // group,),
            in_specs=specs,
            out_specs=pl.BlockSpec((group, rows, half), lambda i, ix, h: (i, 0, 0)),
        ),
        out_shape=jax.ShapeDtypeStruct((count, rows, half), jnp.float32),
        compiler_params=pltpu.CompilerParams(vmem_limit_bytes=48 * 2**20),
    )(index, island.reshape(1), *([own_grad, other] * group))


def split(value):
    high = value.astype(jnp.bfloat16)
    return high, (value - high.astype(jnp.float32)).astype(jnp.bfloat16)


def dot(left, right, axis=0):
    dims = (((1,), (axis,)), ((), ()))
    return lax.dot_general(left, right, dims, preferred_element_type=jnp.float32)


def product(left, right):
    left_high, left_low = split(left)
    right_high, right_low = split(right)
    return dot(left_high, right_high) + (dot(left_high, right_low) + dot(left_low, right_high))


def factor_of(gram):
    on_diagonal = lax.broadcasted_iota(jnp.int32, gram.shape, 0) == lax.broadcasted_iota(jnp.int32, gram.shape, 1)
    squares = jnp.sum(jnp.where(on_diagonal, gram, 0.0), axis=(0, 1), keepdims=True)
    inverse = 1.0 / (jnp.sqrt(squares) + EPSILON)
    scaled_identity = jnp.where(on_diagonal, COEF_A, 0.0)
    start = gram * (inverse * inverse)
    first = scaled_identity + (COEF_B * start + COEF_C * product(start, start))
    second_gram = product(product(first, start), first)
    second = scaled_identity + (COEF_B * second_gram + COEF_C * product(second_gram, second_gram))
    return product(second, first) * inverse


def transport_kernel(
    n, tensors, chunk, chunks, send_ref, a_ref, b_ref, m_ref,
    stage, block, gram, gram_in, part, part_in, total, factor,
    local_sem, out_sem, send_sem, recv_sem, relay_send, relay_recv,
    gram_send, gram_recv, part_send, part_recv, total_send, total_recv,
):
    me = lax.axis_index("dp")
    island = lax.axis_index("island")
    tensor = lax.axis_index("tensor")
    partner = 1 - island
    mesh_ids = pl.DeviceIdType.MESH
    barrier = pltpu.get_barrier_semaphore()
    for d in range(1, n):
        pl.semaphore_signal(barrier, inc=1, device_id={"dp": lax.rem(me + d, n)}, device_id_type=mesh_ids)
    for d in range(1, tensors):
        pl.semaphore_signal(barrier, inc=1, device_id={"tensor": lax.rem(tensor + d, tensors)}, device_id_type=mesh_ids)
    pl.semaphore_signal(barrier, inc=1, device_id={"island": partner}, device_id_type=mesh_ids)
    pl.semaphore_wait(barrier, n + tensors - 1)

    size = gram.shape[1]
    mid = size // 2
    own_rows = pl.ds(pl.multiple_of(island * mid, mid), mid)
    partner_rows = pl.ds(pl.multiple_of(partner * mid, mid), mid)

    def span(c):
        return pl.ds(c * chunk, chunk)

    def remote(c, d):
        peer = lax.rem(me + d, n)
        return pltpu.make_async_remote_copy(
            src_ref=send_ref.at[peer, span(c)],
            dst_ref=a_ref.at[span(c), me],
            send_sem=send_sem.at[c, d],
            recv_sem=recv_sem.at[c, d],
            device_id={"dp": peer},
            device_id_type=mesh_ids,
        )

    def to_partner(source, target, send, recv):
        return pltpu.make_async_remote_copy(
            src_ref=source, dst_ref=target, send_sem=send, recv_sem=recv,
            device_id={"island": partner}, device_id_type=mesh_ids,
        )

    def relay(c):
        return to_partner(a_ref.at[span(c)], b_ref.at[span(c)], relay_send.at[c], relay_recv.at[c])

    def gram_copy(c):
        return to_partner(gram.at[span(c), partner_rows], gram_in.at[span(c)], gram_send.at[c], gram_recv.at[c])

    def total_copy(c):
        rows = total.at[span(c), own_rows]
        return to_partner(rows, rows, total_send.at[c], total_recv.at[c])

    def part_copy(c, d):
        return pltpu.make_async_remote_copy(
            src_ref=part.at[span(c)],
            dst_ref=part_in.at[d - 1, span(c)],
            send_sem=part_send.at[c, d],
            recv_sem=part_recv.at[c, d],
            device_id={"tensor": lax.rem(tensor + d, tensors)},
            device_id_type=mesh_ids,
        )

    def factor_copy(c):
        return pltpu.make_async_copy(factor.at[span(c)], m_ref.at[span(c)], out_sem.at[c])

    def start(c, carry):
        for d in range(1, n):
            remote(c, d).start()
        return carry

    lax.fori_loop(0, chunks, start, 0)
    load = pltpu.make_async_copy(send_ref.at[me], stage, local_sem.at[0])
    load.start()
    load.wait()
    store = pltpu.make_async_copy(stage, a_ref.at[pl.ds(0, chunk * chunks), me], local_sem.at[1])
    store.start()
    store.wait()

    def arrive(c, carry):
        for d in range(1, n):
            remote(c, d).wait_recv()
        relay(c).start()
        fetch = pltpu.make_async_copy(a_ref.at[span(c)], block, local_sem.at[2])
        fetch.start()
        fetch.wait()

        def own_gram(k, inner):
            high, low = split(block[k].reshape(size, block.shape[3]))
            cross = dot(high, low, 1)
            gram[c * chunk + k] = dot(high, high, 1) + (cross + cross.T)
            return inner

        lax.fori_loop(0, chunk, own_gram, 0)
        gram_copy(c).start()
        gram_copy(c).wait_recv()
        part[span(c)] = gram[span(c), own_rows] + gram_in[span(c)]
        for d in range(1, tensors):
            part_copy(c, d).start()
        for d in range(1, tensors):
            part_copy(c, d).wait_recv()
        summed = part[span(c)]
        for d in range(1, tensors):
            summed = summed + part_in[d - 1, span(c)]
        total[span(c), own_rows] = summed
        total_copy(c).start()
        total_copy(c).wait_recv()

        def own_factor(k, inner):
            factor[c * chunk + k] = factor_of(total[c * chunk + k])
            return inner

        lax.fori_loop(0, chunk, own_factor, 0)
        factor_copy(c).start()
        return carry

    lax.fori_loop(0, chunks, arrive, 0)

    def finish(c, carry):
        for d in range(1, n):
            remote(c, d).wait_send()
        for d in range(1, tensors):
            part_copy(c, d).wait_send()
        relay(c).wait()
        gram_copy(c).wait_send()
        total_copy(c).wait_send()
        factor_copy(c).wait()
        return carry

    lax.fori_loop(0, chunks, finish, 0)


def transport(send, most, chunk, tensors, collective_id):
    n, count, rows, half = send.shape
    chunks = count // chunk
    size = n * rows
    shape = jax.ShapeDtypeStruct((most, n, rows, half), jnp.float32)
    anywhere = pl.BlockSpec(memory_space=pl.ANY)
    one_each = pltpu.SemaphoreType.DMA((chunks,))
    return pl.pallas_call(
        functools.partial(transport_kernel, n, tensors, chunk, chunks),
        out_shape=(shape, shape, jax.ShapeDtypeStruct((most, size, size), jnp.float32)),
        in_specs=[anywhere],
        out_specs=(anywhere, anywhere, anywhere),
        scratch_shapes=[
            pltpu.VMEM((count, rows, half), jnp.float32),
            pltpu.VMEM((chunk, n, rows, half), jnp.float32),
            pltpu.VMEM((count, size, size), jnp.float32),
            pltpu.VMEM((count, size // 2, size), jnp.float32),
            pltpu.VMEM((count, size // 2, size), jnp.float32),
            pltpu.VMEM((tensors - 1, count, size // 2, size), jnp.float32),
            pltpu.VMEM((count, size, size), jnp.float32),
            pltpu.VMEM((count, size, size), jnp.float32),
            pltpu.SemaphoreType.DMA((3,)),
            one_each,
            pltpu.SemaphoreType.DMA((chunks, n)),
            pltpu.SemaphoreType.DMA((chunks, n)),
            one_each,
            one_each,
            one_each,
            one_each,
            pltpu.SemaphoreType.DMA((chunks, tensors)),
            pltpu.SemaphoreType.DMA((chunks, tensors)),
            one_each,
            one_each,
        ],
        compiler_params=pltpu.CompilerParams(
            collective_id=collective_id, has_side_effects=True, vmem_limit_bytes=60 * 2**20
        ),
    )(send)


def final_kernel(scale, place_ref, valid_ref, island_ref, m_ref, a_ref, b_ref, out_ref):
    half = a_ref.shape[2]
    valid = valid_ref[pl.program_id(0)] > 0
    island = island_ref[0]
    for source, part in ((a_ref, island), (b_ref, 1 - island)):
        value = scale * product(m_ref[0], source[0])
        columns = pl.ds(pl.multiple_of(part * half, half), half)
        out_ref[0, 0, :, columns] = jnp.where(valid, value, 0.0).astype(jnp.bfloat16)


def finals(factor, mine, partner, place, valid, island, width):
    count = place.shape[0]
    size, half = mine.shape[1], mine.shape[2]
    pick = lambda i, p, v, h: (p[i], 0, 0)
    return pl.pallas_call(
        functools.partial(final_kernel, math.sqrt(width)),
        grid_spec=pltpu.PrefetchScalarGridSpec(
            num_scalar_prefetch=3,
            grid=(count,),
            in_specs=[
                pl.BlockSpec((1, size, size), pick),
                pl.BlockSpec((1, size, half), pick),
                pl.BlockSpec((1, size, half), pick),
            ],
            out_specs=pl.BlockSpec((1, 1, size, 2 * half), lambda i, p, v, h: (0, i, 0, 0)),
        ),
        out_shape=jax.ShapeDtypeStruct((1, count, size, 2 * half), jnp.bfloat16),
        compiler_params=pltpu.CompilerParams(vmem_limit_bytes=48 * 2**20),
    )(place, valid.astype(jnp.int32), island.reshape(1), factor, mine, partner)


def body(pseudo_grad, block_owner):
    own_grad = pseudo_grad[0]
    blocks, rows, columns = own_grad.shape
    half = columns // 2
    dp_count = lax.axis_size("dp")
    island_count = lax.axis_size("island")
    tensors = lax.axis_size("tensor")
    owner_count = island_count * dp_count
    slot_count = 2 * (blocks // owner_count)
    most = island_count * slot_count
    least = blocks // dp_count
    chunk = max(1, slot_count // 4)
    island = lax.axis_index("island")
    device_dp = lax.axis_index("dp")

    slot = rank_before(block_owner)
    chip = lax.rem(block_owner, dp_count)
    chip_slot = rank_before(chip)
    send_index, _ = invert(chip * most + chip_slot, dp_count * most)
    send_index = send_index.reshape(dp_count, most)
    needed = jnp.max(chip_slot) + 1
    own_index, own_valid = invert(block_owner * slot_count + slot, owner_count * slot_count)
    base = (island * dp_count + device_dp) * slot_count
    own_block = lax.dynamic_slice_in_dim(own_index, base, slot_count)
    own_valid = lax.dynamic_slice_in_dim(own_valid, base, slot_count)
    own_place = chip_slot[own_block]

    theirs = lax.dynamic_slice_in_dim(own_grad, (1 - island) * half, half, axis=2)
    other = lax.ppermute(theirs, "island", [(0, 1), (1, 0)])

    counts = [c for c in range(chunk, most + 1, chunk) if c >= least]

    def branch(count, number):
        def run(own_grad, other):
            packed = pack(own_grad, other, send_index[:, :count].reshape(-1), island)
            return transport(packed.reshape(dp_count, count, rows, half), most, chunk, tensors, number)
        return run

    choice = jnp.sum((needed > jnp.array(counts, dtype=jnp.int32)).astype(jnp.int32))
    mine, partner, factor = lax.switch(choice, [branch(c, i) for i, c in enumerate(counts)], own_grad, other)
    mine = mine.reshape(most, dp_count * rows, half)
    partner = partner.reshape(most, dp_count * rows, half)
    return finals(factor, mine, partner, own_place, own_valid, island, columns * tensors)


def solution(mesh):
    in_specs = (P("island", None, "dp", "tensor"), P())
    out_specs = P(("island", "dp"), None, None, "tensor")
    return jax.shard_map(body, mesh=mesh, in_specs=in_specs, out_specs=out_specs, check_vma=False)
```

```python
import functools
import math

import jax
import jax.numpy as jnp
from jax import lax
from jax.experimental import pallas as pl
from jax.experimental.pallas import tpu as pltpu
from jax.sharding import PartitionSpec as P

COEF_A = 3.4445
COEF_B = -4.775
COEF_C = 2.0315
EPSILON = 1e-07


def rank_before(key):
    positions = jnp.arange(key.shape[0], dtype=jnp.int32)
    same = (key[None, :] == key[:, None]) & (positions[None, :] < positions[:, None])
    return jnp.sum(same.astype(jnp.int32), axis=1)


def invert(target, count):
    positions = jnp.arange(target.shape[0], dtype=jnp.int32)
    matches = target[None, :] == jnp.arange(count, dtype=jnp.int32)[:, None]
    return jnp.sum(jnp.where(matches, positions[None, :], 0), axis=1), jnp.any(matches, axis=1)


def pack_kernel(group, index_ref, half_ref, *refs):
    out_ref = refs[-1]
    for g in range(group):
        out_ref[g] = refs[2 * g][0] + refs[2 * g + 1][0]


def pack(own_grad, other, index, island):
    count = index.shape[0]
    rows, half = other.shape[1], other.shape[2]
    group = max(g for g in range(1, 7) if count % g == 0)
    specs = []
    for g in range(group):
        specs.append(pl.BlockSpec((1, rows, half), lambda i, ix, h, g=g: (ix[i * group + g], 0, h[0])))
        specs.append(pl.BlockSpec((1, rows, half), lambda i, ix, h, g=g: (ix[i * group + g], 0, 0)))
    return pl.pallas_call(
        functools.partial(pack_kernel, group),
        grid_spec=pltpu.PrefetchScalarGridSpec(
            num_scalar_prefetch=2,
            grid=(count // group,),
            in_specs=specs,
            out_specs=pl.BlockSpec((group, rows, half), lambda i, ix, h: (i, 0, 0)),
        ),
        out_shape=jax.ShapeDtypeStruct((count, rows, half), jnp.float32),
        compiler_params=pltpu.CompilerParams(vmem_limit_bytes=48 * 2**20),
    )(index, island.reshape(1), *([own_grad, other] * group))


def split(value):
    high = value.astype(jnp.bfloat16)
    return high, (value - high.astype(jnp.float32)).astype(jnp.bfloat16)


def dot(left, right, axis=0):
    dims = (((1,), (axis,)), ((), ()))
    return lax.dot_general(left, right, dims, preferred_element_type=jnp.float32)


def product(left, right):
    left_high, left_low = split(left)
    right_high, right_low = split(right)
    stacked_left = jnp.concatenate([left_high, left_high, left_low], axis=1)
    stacked_right = jnp.concatenate([right_high, right_low, right_high], axis=0)
    return dot(stacked_left, stacked_right)


def factor_of(gram):
    on_diagonal = lax.broadcasted_iota(jnp.int32, gram.shape, 0) == lax.broadcasted_iota(jnp.int32, gram.shape, 1)
    squares = jnp.sum(jnp.where(on_diagonal, gram, 0.0), axis=(0, 1), keepdims=True)
    inverse = 1.0 / (jnp.sqrt(squares) + EPSILON)
    scaled_identity = jnp.where(on_diagonal, COEF_A, 0.0)
    start = gram * (inverse * inverse)
    first = scaled_identity + (COEF_B * start + COEF_C * product(start, start))
    second_gram = product(product(first, start), first)
    second = scaled_identity + (COEF_B * second_gram + COEF_C * product(second_gram, second_gram))
    return product(second, first) * inverse


def exchange_kernel(pieces, grad_ref, out_ref, send_sem, recv_sem):
    partner = 1 - lax.axis_index("island")
    half = out_ref.shape[2]
    step = out_ref.shape[0] // pieces
    barrier = pltpu.get_barrier_semaphore()
    pl.semaphore_signal(barrier, inc=1, device_id={"island": partner}, device_id_type=pl.DeviceIdType.MESH)
    pl.semaphore_wait(barrier, 1)
    columns = pl.ds(pl.multiple_of(partner * half, half), half)
    copies = [
        pltpu.make_async_remote_copy(
            src_ref=grad_ref.at[pl.ds(p * step, step), :, columns],
            dst_ref=out_ref.at[pl.ds(p * step, step)],
            send_sem=send_sem.at[p],
            recv_sem=recv_sem.at[p],
            device_id={"island": partner},
            device_id_type=pl.DeviceIdType.MESH,
        )
        for p in range(pieces)
    ]
    for copy in copies:
        copy.start()
    for copy in copies:
        copy.wait()


def exchange(own_grad):
    blocks, rows, columns = own_grad.shape
    pieces = 4 if blocks % 4 == 0 else 1
    return pl.pallas_call(
        functools.partial(exchange_kernel, pieces),
        out_shape=jax.ShapeDtypeStruct((blocks, rows, columns // 2), jnp.float32),
        in_specs=[pl.BlockSpec(memory_space=pl.ANY)],
        out_specs=pl.BlockSpec(memory_space=pl.ANY),
        scratch_shapes=[pltpu.SemaphoreType.DMA((pieces,)), pltpu.SemaphoreType.DMA((pieces,))],
        compiler_params=pltpu.CompilerParams(collective_id=100, has_side_effects=True),
    )(own_grad)


def transport_kernel(
    n, tensors, chunk, chunks, send_ref, a_ref, b_ref, m_ref,
    stage, block, gram, gram_in, part, part_in, total, factor,
    local_sem, out_sem, send_sem, recv_sem, relay_send, relay_recv,
    gram_send, gram_recv, part_send, part_recv, total_send, total_recv,
):
    me = lax.axis_index("dp")
    island = lax.axis_index("island")
    tensor = lax.axis_index("tensor")
    partner = 1 - island
    mesh_ids = pl.DeviceIdType.MESH
    barrier = pltpu.get_barrier_semaphore()
    for d in range(1, n):
        pl.semaphore_signal(barrier, inc=1, device_id={"dp": lax.rem(me + d, n)}, device_id_type=mesh_ids)
    for d in range(1, tensors):
        pl.semaphore_signal(barrier, inc=1, device_id={"tensor": lax.rem(tensor + d, tensors)}, device_id_type=mesh_ids)
    pl.semaphore_signal(barrier, inc=1, device_id={"island": partner}, device_id_type=mesh_ids)
    pl.semaphore_wait(barrier, n + tensors - 1)

    size = gram.shape[1]
    mid = size // 2
    own_rows = pl.ds(pl.multiple_of(island * mid, mid), mid)
    partner_rows = pl.ds(pl.multiple_of(partner * mid, mid), mid)

    def steps(run):
        bulk = chunks - 1

        def whole(c, carry):
            run((c, c * chunk, chunk))
            return carry

        def single(j, carry):
            run((bulk + j, bulk * chunk + j, 1))
            return carry

        lax.fori_loop(0, bulk, whole, 0)
        lax.fori_loop(0, chunk, single, 0)

    def span(c):
        return pl.ds(c[1], c[2])

    def remote(c, d):
        peer = lax.rem(me + d, n)
        return pltpu.make_async_remote_copy(
            src_ref=send_ref.at[peer, span(c)],
            dst_ref=a_ref.at[span(c), me],
            send_sem=send_sem.at[c[0], d],
            recv_sem=recv_sem.at[c[0], d],
            device_id={"dp": peer},
            device_id_type=mesh_ids,
        )

    def to_partner(source, target, send, recv):
        return pltpu.make_async_remote_copy(
            src_ref=source, dst_ref=target, send_sem=send, recv_sem=recv,
            device_id={"island": partner}, device_id_type=mesh_ids,
        )

    def relay(c):
        return to_partner(a_ref.at[span(c)], b_ref.at[span(c)], relay_send.at[c[0]], relay_recv.at[c[0]])

    def gram_copy(c):
        return to_partner(gram.at[span(c), partner_rows], gram_in.at[span(c)], gram_send.at[c[0]], gram_recv.at[c[0]])

    def total_copy(c):
        rows = total.at[span(c), own_rows]
        return to_partner(rows, rows, total_send.at[c[0]], total_recv.at[c[0]])

    def part_copy(c, d):
        return pltpu.make_async_remote_copy(
            src_ref=part.at[span(c)],
            dst_ref=part_in.at[d - 1, span(c)],
            send_sem=part_send.at[c[0], d],
            recv_sem=part_recv.at[c[0], d],
            device_id={"tensor": lax.rem(tensor + d, tensors)},
            device_id_type=mesh_ids,
        )

    def factor_copy(c):
        return pltpu.make_async_copy(factor.at[span(c)], m_ref.at[span(c)], out_sem.at[c[0]])

    def start(c):
        for d in range(1, n):
            remote(c, d).start()

    steps(start)
    load = pltpu.make_async_copy(send_ref.at[me], stage, local_sem.at[0])
    load.start()
    load.wait()
    store = pltpu.make_async_copy(stage, a_ref.at[pl.ds(0, chunk * chunks), me], local_sem.at[1])
    store.start()
    store.wait()

    def arrive(c):
        for d in range(1, n):
            remote(c, d).wait_recv()
        relay(c).start()
        fetch = pltpu.make_async_copy(a_ref.at[span(c)], block.at[pl.ds(0, c[2])], local_sem.at[2])
        fetch.start()
        fetch.wait()

        def own_gram(k, inner):
            high, low = split(block[k].reshape(size, block.shape[3]))
            cross = dot(high, low, 1)
            gram[c[1] + k] = dot(high, high, 1) + (cross + cross.T)
            return inner

        lax.fori_loop(0, c[2], own_gram, 0)
        gram_copy(c).start()
        gram_copy(c).wait_recv()
        part[span(c)] = gram[span(c), own_rows] + gram_in[span(c)]
        for d in range(1, tensors):
            part_copy(c, d).start()
        for d in range(1, tensors):
            part_copy(c, d).wait_recv()
        summed = part[span(c)]
        for d in range(1, tensors):
            summed = summed + part_in[d - 1, span(c)]
        total[span(c), own_rows] = summed
        total_copy(c).start()
        total_copy(c).wait_recv()

        def own_factor(k, inner):
            factor[c[1] + k] = factor_of(total[c[1] + k])
            return inner

        lax.fori_loop(0, c[2], own_factor, 0)
        factor_copy(c).start()

    steps(arrive)

    def finish(c):
        for d in range(1, n):
            remote(c, d).wait_send()
        for d in range(1, tensors):
            part_copy(c, d).wait_send()
        relay(c).wait()
        gram_copy(c).wait_send()
        total_copy(c).wait_send()
        factor_copy(c).wait()

    steps(finish)


def transport(send, most, chunk, tensors, collective_id):
    n, count, rows, half = send.shape
    chunks = count // chunk
    size = n * rows
    shape = jax.ShapeDtypeStruct((most, n, rows, half), jnp.float32)
    anywhere = pl.BlockSpec(memory_space=pl.ANY)
    one_each = pltpu.SemaphoreType.DMA((chunks - 1 + chunk,))
    return pl.pallas_call(
        functools.partial(transport_kernel, n, tensors, chunk, chunks),
        out_shape=(shape, shape, jax.ShapeDtypeStruct((most, size, size), jnp.float32)),
        in_specs=[anywhere],
        out_specs=(anywhere, anywhere, anywhere),
        scratch_shapes=[
            pltpu.VMEM((count, rows, half), jnp.float32),
            pltpu.VMEM((chunk, n, rows, half), jnp.float32),
            pltpu.VMEM((count, size, size), jnp.float32),
            pltpu.VMEM((count, size // 2, size), jnp.float32),
            pltpu.VMEM((count, size // 2, size), jnp.float32),
            pltpu.VMEM((tensors - 1, count, size // 2, size), jnp.float32),
            pltpu.VMEM((count, size, size), jnp.float32),
            pltpu.VMEM((count, size, size), jnp.float32),
            pltpu.SemaphoreType.DMA((3,)),
            one_each,
            pltpu.SemaphoreType.DMA((chunks - 1 + chunk, n)),
            pltpu.SemaphoreType.DMA((chunks - 1 + chunk, n)),
            one_each,
            one_each,
            one_each,
            one_each,
            pltpu.SemaphoreType.DMA((chunks - 1 + chunk, tensors)),
            pltpu.SemaphoreType.DMA((chunks - 1 + chunk, tensors)),
            one_each,
            one_each,
        ],
        compiler_params=pltpu.CompilerParams(
            collective_id=collective_id, has_side_effects=True, vmem_limit_bytes=60 * 2**20
        ),
    )(send)


def final_kernel(scale, place_ref, valid_ref, island_ref, m_ref, a_ref, b_ref, out_ref):
    half = a_ref.shape[2]
    valid = valid_ref[pl.program_id(0)] > 0
    island = island_ref[0]
    for source, part in ((a_ref, island), (b_ref, 1 - island)):
        value = scale * product(m_ref[0], source[0])
        columns = pl.ds(pl.multiple_of(part * half, half), half)
        out_ref[0, 0, :, columns] = jnp.where(valid, value, 0.0).astype(jnp.bfloat16)


def finals(factor, mine, partner, place, valid, island, width):
    count = place.shape[0]
    size, half = mine.shape[1], mine.shape[2]
    pick = lambda i, p, v, h: (p[i], 0, 0)
    return pl.pallas_call(
        functools.partial(final_kernel, math.sqrt(width)),
        grid_spec=pltpu.PrefetchScalarGridSpec(
            num_scalar_prefetch=3,
            grid=(count,),
            in_specs=[
                pl.BlockSpec((1, size, size), pick),
                pl.BlockSpec((1, size, half), pick),
                pl.BlockSpec((1, size, half), pick),
            ],
            out_specs=pl.BlockSpec((1, 1, size, 2 * half), lambda i, p, v, h: (0, i, 0, 0)),
        ),
        out_shape=jax.ShapeDtypeStruct((1, count, size, 2 * half), jnp.bfloat16),
        compiler_params=pltpu.CompilerParams(vmem_limit_bytes=48 * 2**20),
    )(place, valid.astype(jnp.int32), island.reshape(1), factor, mine, partner)


def body(pseudo_grad, block_owner):
    own_grad = pseudo_grad[0]
    blocks, rows, columns = own_grad.shape
    half = columns // 2
    dp_count = lax.axis_size("dp")
    island_count = lax.axis_size("island")
    tensors = lax.axis_size("tensor")
    owner_count = island_count * dp_count
    slot_count = 2 * (blocks // owner_count)
    most = island_count * slot_count
    least = blocks // dp_count
    chunk = max(1, slot_count // 4)
    island = lax.axis_index("island")
    device_dp = lax.axis_index("dp")

    slot = rank_before(block_owner)
    chip = lax.rem(block_owner, dp_count)
    chip_slot = rank_before(chip)
    send_index, _ = invert(chip * most + chip_slot, dp_count * most)
    send_index = send_index.reshape(dp_count, most)
    needed = jnp.max(chip_slot) + 1
    own_index, own_valid = invert(block_owner * slot_count + slot, owner_count * slot_count)
    base = (island * dp_count + device_dp) * slot_count
    own_block = lax.dynamic_slice_in_dim(own_index, base, slot_count)
    own_valid = lax.dynamic_slice_in_dim(own_valid, base, slot_count)
    own_place = chip_slot[own_block]

    other = exchange(own_grad)

    counts = [c for c in range(chunk, most + 1, chunk) if c >= least]

    def branch(count, number):
        def run(own_grad, other):
            packed = pack(own_grad, other, send_index[:, :count].reshape(-1), island)
            return transport(packed.reshape(dp_count, count, rows, half), most, chunk, tensors, number)
        return run

    choice = jnp.sum((needed > jnp.array(counts, dtype=jnp.int32)).astype(jnp.int32))
    mine, partner, factor = lax.switch(choice, [branch(c, i) for i, c in enumerate(counts)], own_grad, other)
    mine = mine.reshape(most, dp_count * rows, half)
    partner = partner.reshape(most, dp_count * rows, half)
    return finals(factor, mine, partner, own_place, own_valid, island, columns * tensors)


def solution(mesh):
    in_specs = (P("island", None, "dp", "tensor"), P())
    out_specs = P(("island", "dp"), None, None, "tensor")
    return jax.shard_map(body, mesh=mesh, in_specs=in_specs, out_specs=out_specs, check_vma=False)
```
